32 devices in a mesh: pair: 16 (over z, y, x), rep: 2 (over core).
Axes of the slice: x: 2, y: 2, z: 4, core: 2. Of those that a mesh axis runs over, the one named last changes fastest.
Arguments:
- triplet_pairs: int32 [256, 3], P(('pair', 'rep')), may hold values from 0 to 1023, as said below
- tno_width: int32 [256], P(('pair', 'rep')), may hold values from 64 to 128
- pair_width: int32 [1024], P('pair'), may hold values from 32 to 64
- pair_coeff: bfloat16 [1024, 64, 1024], P('pair'), may hold values from -0.1875 to 0.1875
- pair_amps: bfloat16 [1024, 64, 64], P('pair'), may hold values from -0.03125 to 0.03125
- pair_exch: bfloat16 [1024, 64, 64], P('pair'), may hold values from -0.3125 to 0.3125
- tno_coeff: bfloat16 [256, 1024, 128], P(('pair', 'rep')), may hold values from -0.1875 to 0.1875
- int_left: bfloat16 [256, 3, 128, 128], P(('pair', 'rep')), may hold values from -6 to 6
- int_right: bfloat16 [256, 3, 128, 128], P(('pair', 'rep')), may hold values from -6 to 6
- singles: float32 [256, 3, 128], P(('pair', 'rep')), may hold values from -6 to 6
- tno_energy: float32 [256, 128], P(('pair', 'rep')), may hold values from 0.5 to 5
- gap: float32 [256], P(('pair', 'rep')), may hold values from 1 to 4
Outputs:
- triplet_energy: float32 [256], P(('pair', 'rep'))
- pair_energy: float32 [1024], P('pair')
The draws below stay inside these ranges and needn't reach their ends.
Inputs may be any that keep to these rules, and one draw needn't show every extreme that they name: `triplet_pairs`: pair p is owned by index p // 64 of axis pair. The triplets of one chip are rows 2 * c * 8 to 2 * (c + 1) * 8 - 1; among their 48 pair ids at most 3 have one owner, and in every chip some owner has exactly 3 of them.
All inputs are finite; a program needn't handle non-finite values.
Results may differ from the reference program's by a relative error of at most 0.00044.
Values may be sent and summed in bfloat16 or wider, within the bound.
A program may use at most 128 MiB of HBM per device.

```python
import math
import jax
import jax.numpy as jnp
from jax import lax

TRIP_DEV = 8
PAIR_DEV = 64
A = 64
B = 128
DOM = 1024
TRIPLETS = 256
PAIRS = 1024
N_PAIR = 16


def draw_triplet_pairs(key, part):
    references = 6 * TRIP_DEV
    per_owner = (references + N_PAIR - 1) // N_PAIR
    half_len = references // 2

    def one_chip(chip_key):
        key_list = jax.random.split(chip_key, per_owner + 4)
        permuted = jnp.concatenate([jax.random.permutation(key_list[turn], N_PAIR).astype(jnp.int32) for turn in range(per_owner)])
        owners = permuted[:references]
        hottest = permuted[(per_owner - 1) * N_PAIR]
        position = jnp.arange(references, dtype=jnp.int32)
        reorder = jnp.argsort(jnp.where(owners == hottest, 0, references) + position)
        owners = owners[reorder]
        first_half = owners[:half_len][jax.random.permutation(key_list[per_owner], half_len)]
        second_half = owners[half_len:][jax.random.permutation(key_list[per_owner + 1], half_len)]
        flipped = jax.random.randint(key_list[per_owner + 2], (), 0, 2)
        owners = jnp.where(flipped == 1, jnp.concatenate([second_half, first_half]), jnp.concatenate([first_half, second_half]))
        local_rows = jax.random.randint(key_list[per_owner + 3], (references,), 0, PAIR_DEV)
        return (owners * PAIR_DEV + local_rows).astype(jnp.int32)
    pair_ids = jax.vmap(one_chip)(jax.random.split(jax.random.fold_in(key, 7), N_PAIR))
    return pair_ids.reshape(TRIPLETS, 3)


def plant(values, key, smallest, high):
    longest = values.shape.index(max(values.shape))
    spots = []
    for shift in (0, 1):
        where = [jax.random.randint(jax.random.fold_in(key, axis), (), 0, length) for axis, length in enumerate(values.shape)]
        where[longest] = (where[longest] + shift) % values.shape[longest]
        spots.append(tuple(where))
    return values.at[spots[0]].set(smallest).at[spots[1]].set(high)


def level_of(key, shape, cuts, smallest, top_value):
    gain, own = 1.0, jax.random.fold_in(key, 6)
    for dim, parts in cuts:
        draws = jnp.exp(jax.random.uniform(jax.random.fold_in(own, dim), (parts,), jnp.float32, smallest / len(cuts), top_value / len(cuts)))
        gain = gain * jnp.repeat(draws, shape[dim] // parts).reshape([-1 if axis == dim else 1 for axis in range(len(shape))])
    return gain


def centred(own_key, extent, width, bound, cuts=(), kind=jnp.bfloat16):
    entries = width * jax.random.normal(own_key, extent, jnp.float32)
    if cuts:
        entries = entries * level_of(own_key, extent, cuts, -0.22, 0.18)
    return jnp.clip(entries, -bound, bound).astype(kind)


def setup_inputs(seed: int = 0) -> dict:
    keys = jax.random.split(jax.random.key(seed), 13)
    triplet_pairs = draw_triplet_pairs(jax.random.fold_in(keys[12], 71), 0)
    tno_width = plant(jax.random.randint(keys[1], (TRIPLETS,), B // 2, B + 1), jax.random.fold_in(keys[1], 1), B // 2, B).astype(jnp.int32)
    pair_width = plant(jax.random.randint(keys[2], (PAIRS,), A // 2, A + 1), jax.random.fold_in(keys[2], 1), A // 2, A).astype(jnp.int32)
    pair_coeff = centred(keys[3], (PAIRS, A, DOM), DOM ** -0.5, 0.1875, ((0, 16),))
    pair_amps = centred(keys[4], (PAIRS, A, A), (2.0 * DOM / (A * B * B)), 0.03125, ((0, 16),))
    pair_exch = centred(keys[5], (PAIRS, A, A), (20.0 * DOM / (A * B * B)), 0.3125, ((0, 16),))
    tno_coeff = centred(keys[6], (TRIPLETS, DOM, B), DOM ** -0.5, 0.1875, ((0, 32),))
    int_left = centred(keys[7], (TRIPLETS, 3, B, B), 1.0, 6.0, ((0, 32),))
    int_right = centred(keys[8], (TRIPLETS, 3, B, B), 1.0, 6.0, ((0, 32),))
    singles = centred(keys[9], (TRIPLETS, 3, B), 0.5, 6.0, ((0, 32),), jnp.float32)
    tno_energy = jnp.clip(jnp.exp(math.log(5.0) - 2.3025851 * jax.random.uniform(keys[10], (TRIPLETS, B), jnp.float32) ** level_of(keys[10], (TRIPLETS, B), ((0, 32),), -0.2, 0.2)), 0.5, 5.0)
    gap = jnp.clip(jnp.exp(math.log(4.0) - 1.3862944 * jax.random.uniform(keys[11], (TRIPLETS,), jnp.float32) ** level_of(keys[11], (TRIPLETS,), ((0, 32),), -0.2, 0.2)), 1.0, 4.0)
    return dict(triplet_pairs=triplet_pairs, tno_width=tno_width, pair_width=pair_width, pair_coeff=pair_coeff, pair_amps=pair_amps, pair_exch=pair_exch, tno_coeff=tno_coeff, int_left=int_left, int_right=int_right, singles=singles, tno_energy=tno_energy, gap=gap)


def projected_energy(pno_coeff, pno_blocks, tno_block, tno_count, left, right, single_amps, tno_levels, shift):
    tno_size = tno_block.shape[1]
    pno_size = pno_coeff.shape[1]
    kept_cols = (jnp.arange(tno_size, dtype=jnp.int32) < tno_count).astype(jnp.float32)
    tno_kept = tno_block.astype(jnp.float32) * kept_cols[None, :]
    intersection = lax.optimization_barrier(jnp.einsum('xad,db->xab', pno_coeff.astype(jnp.float32), tno_kept).astype(jnp.bfloat16))
    halfway = jnp.einsum('xab,xac->xbc', intersection.astype(jnp.float32), pno_blocks.astype(jnp.float32))
    halfway = lax.optimization_barrier(halfway.astype(jnp.bfloat16)).reshape(3, tno_size, 2, pno_size)
    projected = jnp.einsum('xbkc,xcd->xkbd', halfway.astype(jnp.float32), intersection.astype(jnp.float32))
    amps_tno = lax.optimization_barrier(projected[:, 0].astype(jnp.bfloat16))
    exch_tno = projected[:, 1]
    khatri = left.astype(jnp.float32)[:, :, :, None] * right.astype(jnp.float32)[:, :, None, :]
    khatri = lax.optimization_barrier(khatri.astype(jnp.bfloat16))
    expanded = khatri.reshape(3 * tno_size, tno_size * tno_size)
    leading = jnp.transpose(amps_tno, (1, 0, 2)).reshape(tno_size, 3 * tno_size)
    connected = jnp.dot(leading, expanded, preferred_element_type=jnp.float32).reshape(tno_size, tno_size, tno_size)
    complete = connected + single_amps[0][None, None, :] * exch_tno[0][:, :, None]
    complete = complete + single_amps[1][None, :, None] * exch_tno[1][:, None, :]
    complete = complete + single_amps[2][:, None, None] * exch_tno[2][None, :, :]
    denominator = tno_levels[:, None, None] + tno_levels[None, :, None] + tno_levels[None, None, :] + shift
    cube_mask = kept_cols[:, None, None] * kept_cols[None, :, None] * kept_cols[None, None, :]
    return jnp.sum(cube_mask * connected * complete / denominator)


def reference(triplet_pairs, tno_width, pair_width, pair_coeff, pair_amps, pair_exch, tno_coeff, int_left, int_right, singles, tno_energy, gap):
    kept_rows = (jnp.arange(A, dtype=jnp.int32)[None, :] < pair_width[:, None]).astype(jnp.float32)
    masked = (pair_coeff.astype(jnp.float32) * kept_rows[:, :, None]).astype(jnp.bfloat16)
    paired = jnp.concatenate([pair_amps, pair_exch], axis=2)

    def single_triplet(index):
        pair_ids = triplet_pairs[index]
        return projected_energy(masked[pair_ids], paired[pair_ids], tno_coeff[index], tno_width[index], int_left[index], int_right[index], singles[index], tno_energy[index], gap[index])

    energies = lax.map(single_triplet, jnp.arange(TRIPLETS, dtype=jnp.int32))
    shares = jnp.repeat(energies / 3.0, 3)
    pair_energy = jax.ops.segment_sum(shares, triplet_pairs.reshape(-1), num_segments=PAIRS)
    return energies, pair_energy
```

```python
import functools

import jax
import jax.numpy as jnp
from jax import lax
from jax.experimental import pallas as pl
from jax.experimental.pallas import tpu as pltpu
from jax.sharding import PartitionSpec as P

GROUP = 8


def triplet_kernel(
    pos_ref, width_ref, gap_ref, level_ref, single_ref,
    c0, c1, c2, p0, p1, p2, tno_ref, left_ref, right_ref, sing_ref, energy_ref,
    out_ref, lt_ref, at_ref, rm_ref, base_ref, s2_ref, x0_ref, x1_ref, x2_ref, acc_ref,
):
    t = pl.program_id(0)
    width = width_ref[t]
    pno, tno = c0.shape[1], tno_ref.shape[2]
    kept = lax.broadcasted_iota(jnp.int32, (1, tno), 1) < width
    keep = kept.astype(jnp.float32)
    keep_b = keep.astype(jnp.bfloat16)
    coeff = jnp.concatenate([c0[0], c1[0], c2[0]], axis=0)
    inter = jnp.dot(coeff, tno_ref[0], preferred_element_type=jnp.float32)
    inter = (inter * keep).astype(jnp.bfloat16)
    for x, blocks in enumerate((p0, p1, p2)):
        own = inter[x * pno:(x + 1) * pno]
        half = lax.dot_general(
            own, blocks[0], (((0,), (0,)), ((), ())), preferred_element_type=jnp.float32
        ).astype(jnp.bfloat16)
        amps = jnp.dot(half[:, :pno], own, preferred_element_type=jnp.float32)
        exch = jnp.dot(half[:, pno:], own, preferred_element_type=jnp.float32)
        cols = slice(x * tno, (x + 1) * tno)
        at_ref[:, cols] = amps.astype(jnp.bfloat16)
        (x0_ref, x1_ref, x2_ref)[x][...] = exch
        lt_ref[:, cols] = jnp.transpose(left_ref[0, x].astype(jnp.float32) * keep)
        rm_ref[cols, :] = right_ref[0, x] * keep_b
    levels = energy_ref[0]
    base_ref[...] = (
        jnp.transpose(jnp.broadcast_to(levels, (tno, tno))) + levels + gap_ref[t]
    )
    s2_ref[...] = jnp.transpose(jnp.broadcast_to(sing_ref[0, 2:3], (tno, tno)))
    acc_ref[...] = jnp.zeros_like(acc_ref)

    @pl.loop(0, (width + GROUP - 1) // GROUP)
    def _(g):
        first = pl.multiple_of(g * GROUP, GROUP)
        rows = lt_ref[pl.ds(first, GROUP), :]
        at = at_ref[...]
        scaled = [
            at * jnp.broadcast_to(rows[j:j + 1], at.shape).astype(jnp.bfloat16)
            for j in range(GROUP)
        ]
        conn = jnp.dot(
            jnp.concatenate(scaled, axis=0), rm_ref[...], preferred_element_type=jnp.float32
        )
        x2 = x2_ref[pl.ds(first, GROUP), :]
        x0 = x0_ref[...]
        s0 = sing_ref[0, 0:1]
        total = acc_ref[...]
        for j in range(GROUP):
            part = conn[j * tno:(j + 1) * tno]
            full = part + x0[:, j:j + 1] * s0
            full = full + single_ref[t, first + j] * x1_ref[...]
            full = full + s2_ref[...] * x2[j:j + 1]
            term = part * full / (base_ref[...] + level_ref[t, first + j])
            total = total + jnp.sum(term.reshape(tno // 8, 8, tno), axis=0)
        acc_ref[...] = total
        x0_ref[...] = pltpu.roll(x0, tno - GROUP, 1)

    out_ref[...] = jnp.broadcast_to(jnp.sum(acc_ref[...]), out_ref.shape)


def triplet_energies(
    positions, widths, flat_coeff, flat_paired, tno_coeff, left, right, singles, levels, gap
):
    trips, domain, tno = tno_coeff.shape
    pno = flat_coeff.shape[1]

    def pair_spec(shape, x):
        return pl.BlockSpec((1,) + shape, lambda t, pos, *_: (pos[t * 3 + x], 0, 0))

    def own_spec(shape):
        return pl.BlockSpec((1,) + shape, lambda t, *_: (t,) + (0,) * len(shape))

    out = pl.pallas_call(
        triplet_kernel,
        out_shape=jax.ShapeDtypeStruct((trips, 1, 128), jnp.float32),
        grid_spec=pltpu.PrefetchScalarGridSpec(
            num_scalar_prefetch=5,
            grid=(trips,),
            in_specs=[pair_spec((pno, domain), x) for x in range(3)]
            + [pair_spec((pno, 2 * pno), x) for x in range(3)]
            + [
                own_spec((domain, tno)),
                own_spec((3, tno, tno)),
                own_spec((3, tno, tno)),
                own_spec((3, tno)),
                own_spec((1, tno)),
            ],
            out_specs=own_spec((1, 128)),
            scratch_shapes=[
                pltpu.VMEM((tno, 3 * tno), jnp.float32),
                pltpu.VMEM((tno, 3 * tno), jnp.bfloat16),
                pltpu.VMEM((3 * tno, tno), jnp.bfloat16),
            ]
            + [pltpu.VMEM((tno, tno), jnp.float32)] * 5
            + [pltpu.VMEM((8, tno), jnp.float32)],
        ),
        compiler_params=pltpu.CompilerParams(dimension_semantics=("arbitrary",)),
        name="triplets",
    )(
        positions, widths, gap, levels, singles[:, 1],
        flat_coeff, flat_coeff, flat_coeff, flat_paired, flat_paired, flat_paired,
        tno_coeff, left, right, singles, levels[:, None, :],
    )
    return out[:, 0, 0]


def owner_ranks(owners):
    matching = owners[:, None] == owners[None, :]
    position = jnp.arange(owners.shape[0], dtype=jnp.int32)
    earlier = position[None, :] < position[:, None]
    return jnp.sum(jnp.logical_and(matching, earlier), axis=1)


def body(
    triplet_pairs,
    tno_width,
    pair_width,
    pair_coeff,
    pair_amps,
    pair_exch,
    tno_coeff,
    int_left,
    int_right,
    singles,
    tno_energy,
    gap,
):
    owner_count = lax.axis_size("pair")
    pair_dev = pair_coeff.shape[0]
    pno_size = pair_coeff.shape[1]
    domain = pair_coeff.shape[2]
    references = triplet_pairs.reshape(-1)
    ref_count = references.shape[0]
    capacity = (2 * ref_count + owner_count - 1) // owner_count
    kept_rows = (jnp.arange(pno_size, dtype=jnp.int32)[None, :] < pair_width[:, None]).astype(
        jnp.bfloat16
    )
    masked = pair_coeff * kept_rows[:, :, None]
    paired = jnp.concatenate([pair_amps, pair_exch], axis=2)
    chip_refs = lax.all_gather(references, "rep", axis=0, tiled=True)
    owners = chip_refs // pair_dev
    slot_rank = owner_ranks(owners)
    requests = (
        jnp.zeros((owner_count * capacity,), jnp.int32)
        .at[owners * capacity + slot_rank]
        .set(chip_refs % pair_dev)
    )
    requests = requests.reshape(owner_count, capacity)
    asked_rows = lax.all_to_all(requests, "pair", split_axis=0, concat_axis=0, tiled=True)
    replica = lax.axis_index("rep")
    coeff_part = lax.dynamic_slice_in_dim(masked, replica * (domain // 2), domain // 2, 2)
    paired_part = lax.dynamic_slice_in_dim(paired, replica * pno_size, pno_size, 2)
    got_coeff, got_paired = (
        lax.all_to_all(coeff_part[asked_rows], "pair", split_axis=0, concat_axis=0, tiled=True),
        lax.all_to_all(paired_part[asked_rows], "pair", split_axis=0, concat_axis=0, tiled=True),
    )
    got_coeff, got_paired = (
        lax.all_gather(got_coeff, "rep", axis=3, tiled=True),
        lax.all_gather(got_paired, "rep", axis=3, tiled=True),
    )
    positions = owners * capacity + slot_rank
    positions = lax.dynamic_slice_in_dim(positions, replica * ref_count, ref_count)
    flat_coeff = got_coeff.reshape(-1, pno_size, domain)
    flat_paired = got_paired.reshape(-1, pno_size, 2 * pno_size)
    energies = triplet_energies(
        positions, tno_width, flat_coeff, flat_paired, tno_coeff, int_left, int_right,
        singles, tno_energy, gap,
    )
    shares = jnp.repeat(energies / 3.0, 3)
    all_pairs = jnp.arange(owner_count * pair_dev, dtype=jnp.int32)
    dense = jnp.sum(
        jnp.where(references[:, None] == all_pairs[None, :], shares[:, None], 0.0), axis=0
    )
    owned = lax.psum_scatter(dense, "pair", scatter_dimension=0, tiled=True)
    pair_energy = lax.psum(owned, "rep")
    return (energies, pair_energy)


def solution(mesh):
    placed = (
        P(("pair", "rep"), None),
        P(("pair", "rep")),
        P("pair"),
        P("pair", None, None),
        P("pair", None, None),
        P("pair", None, None),
        P(("pair", "rep"), None, None),
        P(("pair", "rep"), None, None, None),
        P(("pair", "rep"), None, None, None),
        P(("pair", "rep"), None, None),
        P(("pair", "rep"), None),
        P(("pair", "rep")),
    )
    return jax.shard_map(
        body, mesh=mesh, in_specs=placed, out_specs=(P(("pair", "rep")), P("pair")), check_vma=False
    )
```

```python
import functools

import jax
import jax.numpy as jnp
from jax import lax
from jax.experimental import pallas as pl
from jax.experimental.pallas import tpu as pltpu
from jax.sharding import PartitionSpec as P

GROUP = 8


def triplet_kernel(
    pos_ref, width_ref, gap_ref, level_ref, single_ref,
    c0, c1, c2, p0, p1, p2, tno_ref, left_ref, right_ref, sing_ref, energy_ref,
    out_ref, lt_ref, at_ref, rm_ref, base_ref, s2_ref, x0_ref, x1_ref, x2_ref, acc_ref,
):
    t = pl.program_id(0)
    width = width_ref[t]
    pno, tno = c0.shape[2], tno_ref.shape[2]
    half_dom = c0.shape[3]
    kept = lax.broadcasted_iota(jnp.int32, (1, tno), 1) < width
    keep = kept.astype(jnp.float32)
    keep_b = keep.astype(jnp.bfloat16)
    inter = sum(
        jnp.dot(
            jnp.concatenate([c0[h, 0], c1[h, 0], c2[h, 0]], axis=0),
            tno_ref[0, h * half_dom:(h + 1) * half_dom],
            preferred_element_type=jnp.float32,
        )
        for h in range(2)
    )
    inter = (inter * keep).astype(jnp.bfloat16)
    for x, blocks in enumerate((p0, p1, p2)):
        own = inter[x * pno:(x + 1) * pno]
        pair = jnp.concatenate(
            [
                jnp.concatenate([blocks[h, 0, :, :pno], blocks[h, 0, :, pno:]], axis=0)
                for h in range(2)
            ],
            axis=1,
        )
        half = lax.dot_general(
            own, pair, (((0,), (0,)), ((), ())), preferred_element_type=jnp.float32
        ).astype(jnp.bfloat16)
        amps = jnp.dot(half[:, :pno], own, preferred_element_type=jnp.float32)
        exch = jnp.dot(half[:, pno:], own, preferred_element_type=jnp.float32)
        cols = slice(x * tno, (x + 1) * tno)
        at_ref[:, cols] = amps.astype(jnp.bfloat16)
        (x0_ref, x1_ref, x2_ref)[x][...] = exch
        lt_ref[:, cols] = jnp.transpose(left_ref[0, x].astype(jnp.float32) * keep)
        rm_ref[cols, :] = right_ref[0, x] * keep_b
    levels = energy_ref[0]
    base_ref[...] = (
        jnp.transpose(jnp.broadcast_to(levels, (tno, tno))) + levels + gap_ref[t]
    )
    s2_ref[...] = jnp.transpose(jnp.broadcast_to(sing_ref[0, 2:3], (tno, tno)))
    acc_ref[...] = jnp.zeros_like(acc_ref)

    @pl.loop(0, (width + GROUP - 1) // GROUP)
    def _(g):
        first = pl.multiple_of(g * GROUP, GROUP)
        rows = lt_ref[pl.ds(first, GROUP), :]
        at = at_ref[...]
        scaled = [
            at * jnp.broadcast_to(rows[j:j + 1], at.shape).astype(jnp.bfloat16)
            for j in range(GROUP)
        ]
        conn = jnp.dot(
            jnp.concatenate(scaled, axis=0), rm_ref[...], preferred_element_type=jnp.float32
        )
        x2 = x2_ref[pl.ds(first, GROUP), :]
        x0 = x0_ref[...]
        s0 = sing_ref[0, 0:1]
        total = acc_ref[...]
        for j in range(GROUP):
            part = conn[j * tno:(j + 1) * tno]
            full = part + x0[:, j:j + 1] * s0
            full = full + single_ref[t, first + j] * x1_ref[...]
            full = full + s2_ref[...] * x2[j:j + 1]
            term = part * full / (base_ref[...] + level_ref[t, first + j])
            total = total + jnp.sum(term.reshape(tno // 8, 8, tno), axis=0)
        acc_ref[...] = total
        x0_ref[...] = pltpu.roll(x0, tno - GROUP, 1)

    out_ref[...] = jnp.broadcast_to(jnp.sum(acc_ref[...]), out_ref.shape)


def triplet_energies(
    positions, widths, flat_coeff, flat_paired, tno_coeff, left, right, singles, levels, gap
):
    trips, domain, tno = tno_coeff.shape
    pno = flat_coeff.shape[2]

    def pair_spec(shape, x):
        return pl.BlockSpec((2, 1) + shape, lambda t, pos, *_: (0, pos[t * 3 + x], 0, 0))

    def own_spec(shape):
        return pl.BlockSpec((1,) + shape, lambda t, *_: (t,) + (0,) * len(shape))

    out = pl.pallas_call(
        triplet_kernel,
        out_shape=jax.ShapeDtypeStruct((trips, 1, 128), jnp.float32),
        grid_spec=pltpu.PrefetchScalarGridSpec(
            num_scalar_prefetch=5,
            grid=(trips,),
            in_specs=[pair_spec((pno, domain // 2), x) for x in range(3)]
            + [pair_spec((pno // 2, 2 * pno), x) for x in range(3)]
            + [
                own_spec((domain, tno)),
                own_spec((3, tno, tno)),
                own_spec((3, tno, tno)),
                own_spec((3, tno)),
                own_spec((1, tno)),
            ],
            out_specs=own_spec((1, 128)),
            scratch_shapes=[
                pltpu.VMEM((tno, 3 * tno), jnp.float32),
                pltpu.VMEM((tno, 3 * tno), jnp.bfloat16),
                pltpu.VMEM((3 * tno, tno), jnp.bfloat16),
            ]
            + [pltpu.VMEM((tno, tno), jnp.float32)] * 5
            + [pltpu.VMEM((8, tno), jnp.float32)],
        ),
        compiler_params=pltpu.CompilerParams(dimension_semantics=("arbitrary",)),
        name="triplets",
    )(
        positions, widths, gap, levels, singles[:, 1],
        flat_coeff, flat_coeff, flat_coeff, flat_paired, flat_paired, flat_paired,
        tno_coeff, left, right, singles, levels[:, None, :],
    )
    return out[:, 0]


MESH = pl.DeviceIdType.MESH


def share_kernel(count, reps, x_ref, out_ref, send_sem, recv_sem):
    me = lax.axis_index("pair") * reps + lax.axis_index("rep")
    barrier = pltpu.get_barrier_semaphore()

    @pl.loop(1, count)
    def _(d):
        other = lax.rem(me + d, count)
        pl.semaphore_signal(
            barrier, inc=1, device_id=(other // reps, lax.rem(other, reps)), device_id_type=MESH
        )

    pl.semaphore_wait(barrier, count - 1)

    def copy(d):
        other = lax.rem(me + d, count)
        return pltpu.make_async_remote_copy(
            src_ref=x_ref,
            dst_ref=out_ref.at[me],
            send_sem=send_sem.at[d - 1],
            recv_sem=recv_sem.at[d - 1],
            device_id=(other // reps, lax.rem(other, reps)),
            device_id_type=MESH,
        )

    @pl.loop(1, count)
    def _(d):
        copy(d).start()

    out_ref[me] = x_ref[...]

    @pl.loop(1, count)
    def _(d):
        copy(d).wait()


def share(block, cid):
    owners, reps = lax.axis_size("pair"), lax.axis_size("rep")
    count = owners * reps
    return pl.pallas_call(
        functools.partial(share_kernel, count, reps),
        out_shape=jax.ShapeDtypeStruct((count,) + block.shape, block.dtype),
        in_specs=[pl.BlockSpec(memory_space=pltpu.VMEM)],
        out_specs=pl.BlockSpec(memory_space=pltpu.VMEM),
        scratch_shapes=[
            pltpu.SemaphoreType.DMA((count - 1,)),
            pltpu.SemaphoreType.DMA((count - 1,)),
        ],
        compiler_params=pltpu.CompilerParams(collective_id=cid, has_side_effects=True),
        name="share" + str(cid),
    )(block)


def exchange_kernel(
    count, coeff_ref, block_ref, got_coeff, got_block,
    keep_coeff, keep_block, send_sem, recv_sem, pass_sem, land_sem, local_sem,
):
    me, rep = lax.axis_index("pair"), lax.axis_index("rep")
    sibling = (me, 1 - rep)
    barrier = pltpu.get_barrier_semaphore()
    pl.semaphore_signal(barrier, inc=1, device_id=sibling, device_id_type=MESH)

    @pl.loop(1, count)
    def _(d):
        pl.semaphore_signal(
            barrier, inc=1, device_id=(lax.rem(me + d, count), rep), device_id_type=MESH
        )

    pl.semaphore_wait(barrier, count)

    def send(d, k):
        other = lax.rem(me + d, count)
        return pltpu.make_async_remote_copy(
            src_ref=(coeff_ref, block_ref)[k].at[other],
            dst_ref=(got_coeff, got_block)[k].at[rep, me],
            send_sem=send_sem.at[k, d - 1],
            recv_sem=recv_sem.at[k, d - 1],
            device_id=(other, rep),
            device_id_type=MESH,
        )

    def forward(d, k):
        origin = lax.rem(me - d + count, count)
        return pltpu.make_async_remote_copy(
            src_ref=(got_coeff, got_block)[k].at[rep, origin],
            dst_ref=(got_coeff, got_block)[k].at[rep, origin],
            send_sem=pass_sem.at[k, d],
            recv_sem=land_sem.at[k, d],
            device_id=sibling,
            device_id_type=MESH,
        )

    far_first = sorted(range(1, count), key=lambda d: (-min(d, count - d), d))
    for d in far_first:
        for k in (1, 0):
            send(d, k).start()

    own = []
    for k in range(2):
        source, held = (coeff_ref, block_ref)[k], (keep_coeff, keep_block)[k]
        target = (got_coeff, got_block)[k]
        own.append((
            pltpu.make_async_copy(source.at[me], held, local_sem.at[k, 0]),
            pltpu.make_async_copy(held, target.at[rep, me], local_sem.at[k, 1]),
        ))
    for load, _ in own:
        load.start()
    for load, store in own:
        load.wait()
        store.start()
    for _, store in own:
        store.wait()
    for k in range(2):
        forward(0, k).start()
    for d in far_first[::-1]:
        for k in (1, 0):
            send(d, k).wait_recv()
            forward(d, k).start()

    @pl.loop(1, count)
    def _(d):
        for k in range(2):
            send(d, k).wait_send()

    @pl.loop(0, count)
    def _(d):
        for k in range(2):
            forward(d, k).wait()


def exchange(coeff, block, cid):
    count = coeff.shape[0]
    shapes = [jax.ShapeDtypeStruct((2,) + a.shape, a.dtype) for a in (coeff, block)]
    return pl.pallas_call(
        functools.partial(exchange_kernel, count),
        out_shape=shapes,
        in_specs=[pl.BlockSpec(memory_space=pl.ANY)] * 2,
        out_specs=[pl.BlockSpec(memory_space=pl.ANY)] * 2,
        scratch_shapes=[
            pltpu.VMEM(coeff.shape[1:], coeff.dtype),
            pltpu.VMEM(block.shape[1:], block.dtype),
            pltpu.SemaphoreType.DMA((2, count - 1)),
            pltpu.SemaphoreType.DMA((2, count - 1)),
            pltpu.SemaphoreType.DMA((2, count)),
            pltpu.SemaphoreType.DMA((2, count)),
            pltpu.SemaphoreType.DMA((2, 2)),
        ],
        compiler_params=pltpu.CompilerParams(collective_id=cid, has_side_effects=True),
        name="exchange",
    )(coeff, block)


def gather_kernel(row_ref, rep_ref, coeff_ref, out_ref, held, in_sem, out_sem):
    total, _, half = held.shape
    start = pl.multiple_of(rep_ref[0] * half, half)

    def load(i):
        return pltpu.make_async_copy(
            coeff_ref.at[row_ref[i], :, pl.ds(start, half)], held.at[i], in_sem.at[i]
        )

    def store(i):
        return pltpu.make_async_copy(held.at[i], out_ref.at[i], out_sem.at[i])

    @pl.loop(0, total)
    def _(i):
        load(i).start()

    @pl.loop(0, total)
    def _(i):
        load(i).wait()
        store(i).start()

    @pl.loop(0, total)
    def _(i):
        store(i).wait()


def gather_rows(coeff, rows, rep):
    _, pno, domain = coeff.shape
    total = rows.shape[0]
    return pl.pallas_call(
        gather_kernel,
        out_shape=jax.ShapeDtypeStruct((total, pno, domain // 2), coeff.dtype),
        grid_spec=pltpu.PrefetchScalarGridSpec(
            num_scalar_prefetch=2,
            grid=(),
            in_specs=[pl.BlockSpec(memory_space=pl.ANY)],
            out_specs=pl.BlockSpec(memory_space=pl.ANY),
            scratch_shapes=[
                pltpu.VMEM((total, pno, domain // 2), coeff.dtype),
                pltpu.SemaphoreType.DMA((total,)),
                pltpu.SemaphoreType.DMA((total,)),
            ],
        ),
        name="gather_rows",
    )(rows, rep.reshape(1), coeff)


def body(
    triplet_pairs,
    tno_width,
    pair_width,
    pair_coeff,
    pair_amps,
    pair_exch,
    tno_coeff,
    int_left,
    int_right,
    singles,
    tno_energy,
    gap,
):
    owner_count = lax.axis_size("pair")
    replica, me = lax.axis_index("rep"), lax.axis_index("pair")
    pair_dev, pno, domain = pair_coeff.shape
    trips, tno = tno_coeff.shape[0], tno_coeff.shape[2]
    ref_count = 3 * trips
    capacity = (2 * ref_count + owner_count - 1) // owner_count

    padded = jnp.pad(triplet_pairs, ((0, 0), (0, 128 - 3)))
    shared = share(padded, 0)[:, :, :3]
    ids = shared.reshape(owner_count, 2 * ref_count)
    mine = (ids // pair_dev == me).astype(jnp.float32)
    spot = jnp.arange(2 * ref_count, dtype=jnp.int32)
    before = (spot[:, None] < spot[None, :]).astype(jnp.float32)
    rank = jnp.dot(mine, before)
    slots = jnp.arange(capacity, dtype=jnp.int32).astype(jnp.float32)
    chosen = (mine[:, None, :] > 0) & (rank[:, None, :] == slots[None, :, None])
    rows = jnp.sum(jnp.where(chosen, (ids % pair_dev)[:, None, :], 0), axis=2).reshape(-1)

    inside = jnp.arange(pno, dtype=jnp.int32)[None, :] < pair_width[:, None]
    square = inside[:, :, None] & inside[:, None, :]
    block = jnp.where(square, jnp.where(replica == 0, pair_amps, pair_exch), 0)
    block = jnp.concatenate([block[:, :pno // 2], block[:, pno // 2:]], axis=2)
    send_block = block[rows].reshape(owner_count, capacity, pno // 2, 2 * pno)
    send_coeff = gather_rows(pair_coeff, rows, replica)
    send_coeff = send_coeff.reshape(owner_count, capacity, pno, domain // 2)
    got_coeff, got_block = exchange(send_coeff, send_block, 1)

    chip_refs = lax.dynamic_index_in_dim(ids, me, 0, keepdims=False)
    owners = chip_refs // pair_dev
    earlier = (owners[:, None] == owners[None, :]) & (spot[None, :] < spot[:, None])
    positions = owners * capacity + jnp.sum(earlier.astype(jnp.int32), axis=1)
    positions = lax.dynamic_slice_in_dim(positions, replica * ref_count, ref_count)
    energies = triplet_energies(
        positions,
        tno_width,
        got_coeff.reshape(2, -1, pno, domain // 2),
        got_block.reshape(2, -1, pno // 2, 2 * pno),
        tno_coeff, int_left, int_right, singles, tno_energy, gap,
    )
    everyone = share(energies, 2)[:, :, 0].reshape(-1)
    owned = jnp.arange(pair_dev, dtype=jnp.int32) + me * pair_dev
    shares = jnp.repeat(everyone / 3.0, 3)
    pair_energy = jnp.sum(
        jnp.where(ids.reshape(-1)[None, :] == owned[:, None], shares[None, :], 0.0), axis=1
    )
    return (energies[:, 0], pair_energy)


def solution(mesh):
    placed = (
        P(("pair", "rep"), None),
        P(("pair", "rep")),
        P("pair"),
        P("pair", None, None),
        P("pair", None, None),
        P("pair", None, None),
        P(("pair", "rep"), None, None),
        P(("pair", "rep"), None, None, None),
        P(("pair", "rep"), None, None, None),
        P(("pair", "rep"), None, None),
        P(("pair", "rep"), None),
        P(("pair", "rep")),
    )
    return jax.shard_map(
        body, mesh=mesh, in_specs=placed, out_specs=(P(("pair", "rep")), P("pair")), check_vma=False
    )
```

```python
import functools

import jax
import jax.numpy as jnp
from jax import lax
from jax.experimental import pallas as pl
from jax.experimental.pallas import tpu as pltpu
from jax.sharding import PartitionSpec as P

GROUP = 8
ROW_STEP = 16


def triplet_kernel(
    pos_ref, width_ref, gap_ref, level_ref, single_ref,
    c0, c1, c2, p0, p1, p2, tno_ref, left_ref, right_ref, sing_ref, energy_ref,
    out_ref, lt_ref, at_ref, rm_ref, base_ref, s2_ref, x0_ref, x1_ref, x2_ref, acc_ref,
):
    t = pl.program_id(0)
    width = width_ref[t]
    pno, tno = c0.shape[2], tno_ref.shape[2]
    half_dom = c0.shape[3]
    kept = lax.broadcasted_iota(jnp.int32, (1, tno), 1) < width
    keep = kept.astype(jnp.float32)
    keep_b = keep.astype(jnp.bfloat16)
    inter = sum(
        jnp.dot(
            jnp.concatenate([c0[h, 0], c1[h, 0], c2[h, 0]], axis=0),
            tno_ref[0, h * half_dom:(h + 1) * half_dom],
            preferred_element_type=jnp.float32,
        )
        for h in range(2)
    )
    inter = (inter * keep).astype(jnp.bfloat16)
    for x, blocks in enumerate((p0, p1, p2)):
        own = inter[x * pno:(x + 1) * pno]
        pair = jnp.concatenate(
            [
                jnp.concatenate([blocks[h, 0, :, :pno], blocks[h, 0, :, pno:]], axis=0)
                for h in range(2)
            ],
            axis=1,
        )
        half = lax.dot_general(
            own, pair, (((0,), (0,)), ((), ())), preferred_element_type=jnp.float32
        ).astype(jnp.bfloat16)
        amps = jnp.dot(half[:, :pno], own, preferred_element_type=jnp.float32)
        exch = jnp.dot(half[:, pno:], own, preferred_element_type=jnp.float32)
        cols = slice(x * tno, (x + 1) * tno)
        at_ref[:, cols] = amps.astype(jnp.bfloat16)
        (x0_ref, x1_ref, x2_ref)[x][...] = exch
        lt_ref[:, cols] = jnp.transpose(left_ref[0, x].astype(jnp.float32) * keep)
        rm_ref[cols, :] = right_ref[0, x] * keep_b
    levels = energy_ref[0]
    base_ref[...] = (
        jnp.transpose(jnp.broadcast_to(levels, (tno, tno))) + levels + gap_ref[t]
    )
    s2_ref[...] = jnp.transpose(jnp.broadcast_to(sing_ref[0, 2:3], (tno, tno)))
    acc_ref[...] = jnp.zeros_like(acc_ref)

    for low in range(tno // 2, tno + 1, ROW_STEP):
        fits = width <= low
        if low > tno // 2:
            fits = fits & (width > low - ROW_STEP)

        @pl.when(fits)
        def _(low=low):
            contract(
                low, t, width, level_ref, single_ref, sing_ref, lt_ref, at_ref, rm_ref,
                base_ref, s2_ref, x0_ref, x1_ref, x2_ref, acc_ref,
            )

    @pl.when(t == 0)
    def _():
        out_ref[...] = jnp.zeros_like(out_ref)

    here = lax.broadcasted_iota(jnp.int32, out_ref.shape, 1) == t
    out_ref[...] = jnp.where(here, jnp.sum(acc_ref[...]), out_ref[...])


def contract(
    low, t, width, level_ref, single_ref, sing_ref, lt_ref, at_ref, rm_ref,
    base_ref, s2_ref, x0_ref, x1_ref, x2_ref, acc_ref,
):
    tno = rm_ref.shape[1]

    @pl.loop(0, (width + GROUP - 1) // GROUP)
    def _(g):
        first = pl.multiple_of(g * GROUP, GROUP)
        rows = lt_ref[pl.ds(first, GROUP), :]
        at = at_ref[:low]
        scaled = [
            at * jnp.broadcast_to(rows[j:j + 1], at.shape).astype(jnp.bfloat16)
            for j in range(GROUP)
        ]
        conn = jnp.dot(
            jnp.concatenate(scaled, axis=0), rm_ref[...], preferred_element_type=jnp.float32
        )
        x2 = x2_ref[pl.ds(first, GROUP), :]
        x0 = x0_ref[:low]
        s0 = sing_ref[0, 0:1]
        total = acc_ref[...]

        def pieces(j):
            part = conn[j * low:(j + 1) * low]
            full = part + x0[:, j:j + 1] * s0
            full = full + single_ref[t, first + j] * x1_ref[:low]
            full = full + s2_ref[:low] * x2[j:j + 1]
            return part * full, base_ref[:low] + level_ref[t, first + j]

        for j in range(0, GROUP, 2):
            top, low_den = pieces(j)
            other, other_den = pieces(j + 1)
            term = (top * other_den + other * low_den) / (low_den * other_den)
            total = total + jnp.sum(term.reshape(low // 8, 8, tno), axis=0)
        acc_ref[...] = total
        x0_ref[:low] = pltpu.roll(x0, tno - GROUP, 1)


def padded_to(size):
    return (size + 127) // 128 * 128


def triplet_energies(
    positions, widths, flat_coeff, flat_paired, tno_coeff, left, right, singles, levels, gap
):
    trips, domain, tno = tno_coeff.shape
    pno = flat_coeff.shape[2]

    def pair_spec(shape, x):
        return pl.BlockSpec((2, 1) + shape, lambda t, pos, *_: (0, pos[t * 3 + x], 0, 0))

    def own_spec(shape):
        return pl.BlockSpec((1,) + shape, lambda t, *_: (t,) + (0,) * len(shape))

    out = pl.pallas_call(
        triplet_kernel,
        out_shape=jax.ShapeDtypeStruct((1, padded_to(trips)), jnp.float32),
        grid_spec=pltpu.PrefetchScalarGridSpec(
            num_scalar_prefetch=5,
            grid=(trips,),
            in_specs=[pair_spec((pno, domain // 2), x) for x in range(3)]
            + [pair_spec((pno // 2, 2 * pno), x) for x in range(3)]
            + [
                own_spec((domain, tno)),
                own_spec((3, tno, tno)),
                own_spec((3, tno, tno)),
                own_spec((3, tno)),
                own_spec((1, tno)),
            ],
            out_specs=pl.BlockSpec((1, padded_to(trips)), lambda t, *_: (0, 0)),
            scratch_shapes=[
                pltpu.VMEM((tno, 3 * tno), jnp.float32),
                pltpu.VMEM((tno, 3 * tno), jnp.bfloat16),
                pltpu.VMEM((3 * tno, tno), jnp.bfloat16),
            ]
            + [pltpu.VMEM((tno, tno), jnp.float32)] * 5
            + [pltpu.VMEM((8, tno), jnp.float32)],
        ),
        compiler_params=pltpu.CompilerParams(dimension_semantics=("arbitrary",)),
        name="triplets",
    )(
        positions, widths, gap, levels, singles[:, 1],
        flat_coeff, flat_coeff, flat_coeff, flat_paired, flat_paired, flat_paired,
        tno_coeff, left, right, singles, levels[:, None, :],
    )
    return out


MESH = pl.DeviceIdType.MESH


def share_kernel(count, reps, x_ref, out_ref, send_sem, recv_sem):
    me = lax.axis_index("pair") * reps + lax.axis_index("rep")
    barrier = pltpu.get_barrier_semaphore()

    @pl.loop(1, count)
    def _(d):
        other = lax.rem(me + d, count)
        pl.semaphore_signal(
            barrier, inc=1, device_id=(other // reps, lax.rem(other, reps)), device_id_type=MESH
        )

    pl.semaphore_wait(barrier, count - 1)

    def copy(d):
        other = lax.rem(me + d, count)
        return pltpu.make_async_remote_copy(
            src_ref=x_ref,
            dst_ref=out_ref.at[me],
            send_sem=send_sem.at[d - 1],
            recv_sem=recv_sem.at[d - 1],
            device_id=(other // reps, lax.rem(other, reps)),
            device_id_type=MESH,
        )

    @pl.loop(1, count)
    def _(d):
        copy(d).start()

    out_ref[me] = x_ref[...]

    @pl.loop(1, count)
    def _(d):
        copy(d).wait()


def share(block, cid):
    owners, reps = lax.axis_size("pair"), lax.axis_size("rep")
    count = owners * reps
    return pl.pallas_call(
        functools.partial(share_kernel, count, reps),
        out_shape=jax.ShapeDtypeStruct((count,) + block.shape, block.dtype),
        in_specs=[pl.BlockSpec(memory_space=pltpu.VMEM)],
        out_specs=pl.BlockSpec(memory_space=pltpu.VMEM),
        scratch_shapes=[
            pltpu.SemaphoreType.DMA((count - 1,)),
            pltpu.SemaphoreType.DMA((count - 1,)),
        ],
        compiler_params=pltpu.CompilerParams(collective_id=cid, has_side_effects=True),
        name="share" + str(cid),
    )(block)


def partner(me, d, count, sign=1):
    if count & (count - 1):
        return lax.rem(me + sign * d + count, count)
    other, bit = me, 1
    while bit < count:
        if d & bit:
            other = other + bit * (1 - 2 * lax.rem(me // bit, 2))
        bit *= 2
    return other


def exchange_kernel(
    count, coeff_ref, block_ref, got_coeff, got_block,
    keep_coeff, keep_block, send_sem, recv_sem, pass_sem, land_sem, local_sem,
):
    me, rep = lax.axis_index("pair"), lax.axis_index("rep")
    sibling = (me, 1 - rep)
    barrier = pltpu.get_barrier_semaphore()
    pl.semaphore_signal(barrier, inc=1, device_id=sibling, device_id_type=MESH)

    @pl.loop(1, count)
    def _(d):
        pl.semaphore_signal(
            barrier, inc=1, device_id=(lax.rem(me + d, count), rep), device_id_type=MESH
        )

    pl.semaphore_wait(barrier, count)

    def send(d, k):
        other = partner(me, d, count)
        return pltpu.make_async_remote_copy(
            src_ref=(coeff_ref, block_ref)[k].at[other],
            dst_ref=(got_coeff, got_block)[k].at[rep, me],
            send_sem=send_sem.at[k, d - 1],
            recv_sem=recv_sem.at[k, d - 1],
            device_id=(other, rep),
            device_id_type=MESH,
        )

    def forward(d, k):
        origin = partner(me, d, count, -1)
        return pltpu.make_async_remote_copy(
            src_ref=(got_coeff, got_block)[k].at[rep, origin],
            dst_ref=(got_coeff, got_block)[k].at[rep, origin],
            send_sem=pass_sem.at[k, d],
            recv_sem=land_sem.at[k, d],
            device_id=sibling,
            device_id_type=MESH,
        )

    far_first = list(range(count - 1, 0, -1))
    for d in far_first:
        for k in (1, 0):
            send(d, k).start()

    own = []
    for k in range(2):
        source, held = (coeff_ref, block_ref)[k], (keep_coeff, keep_block)[k]
        target = (got_coeff, got_block)[k]
        own.append((
            pltpu.make_async_copy(source.at[me], held, local_sem.at[k, 0]),
            pltpu.make_async_copy(held, target.at[rep, me], local_sem.at[k, 1]),
        ))
    for load, _ in own:
        load.start()
    for load, store in own:
        load.wait()
        store.start()
    for _, store in own:
        store.wait()
    for k in range(2):
        forward(0, k).start()
    for d in far_first[::-1]:
        for k in (1, 0):
            send(d, k).wait_recv()
            forward(d, k).start()

    for d in range(count):
        for k in range(2):
            if d:
                send(d, k).wait_send()
            forward(d, k).wait()


def exchange(coeff, block, cid):
    count = coeff.shape[0]
    shapes = [jax.ShapeDtypeStruct((2,) + a.shape, a.dtype) for a in (coeff, block)]
    return pl.pallas_call(
        functools.partial(exchange_kernel, count),
        out_shape=shapes,
        in_specs=[pl.BlockSpec(memory_space=pl.ANY)] * 2,
        out_specs=[pl.BlockSpec(memory_space=pl.ANY)] * 2,
        scratch_shapes=[
            pltpu.VMEM(coeff.shape[1:], coeff.dtype),
            pltpu.VMEM(block.shape[1:], block.dtype),
            pltpu.SemaphoreType.DMA((2, count - 1)),
            pltpu.SemaphoreType.DMA((2, count - 1)),
            pltpu.SemaphoreType.DMA((2, count)),
            pltpu.SemaphoreType.DMA((2, count)),
            pltpu.SemaphoreType.DMA((2, 2)),
        ],
        compiler_params=pltpu.CompilerParams(collective_id=cid, has_side_effects=True),
        name="exchange",
    )(coeff, block)


def gather_kernel(row_ref, rep_ref, coeff_ref, out_ref, held, in_sem, out_sem):
    total, _, half = held.shape
    start = pl.multiple_of(rep_ref[0] * half, half)

    def load(i):
        return pltpu.make_async_copy(
            coeff_ref.at[row_ref[i], :, pl.ds(start, half)], held.at[i], in_sem.at[i]
        )

    def store(i):
        return pltpu.make_async_copy(held.at[i], out_ref.at[i], out_sem.at[i])

    @pl.loop(0, total)
    def _(i):
        load(i).start()

    @pl.loop(0, total)
    def _(i):
        load(i).wait()
        store(i).start()

    @pl.loop(0, total)
    def _(i):
        store(i).wait()


def gather_rows(coeff, rows, rep):
    _, pno, domain = coeff.shape
    total = rows.shape[0]
    return pl.pallas_call(
        gather_kernel,
        out_shape=jax.ShapeDtypeStruct((total, pno, domain // 2), coeff.dtype),
        grid_spec=pltpu.PrefetchScalarGridSpec(
            num_scalar_prefetch=2,
            grid=(),
            in_specs=[pl.BlockSpec(memory_space=pl.ANY)],
            out_specs=pl.BlockSpec(memory_space=pl.ANY),
            scratch_shapes=[
                pltpu.VMEM((total, pno, domain // 2), coeff.dtype),
                pltpu.SemaphoreType.DMA((total,)),
                pltpu.SemaphoreType.DMA((total,)),
            ],
        ),
        name="gather_rows",
    )(rows, rep.reshape(1), coeff)


def body(
    triplet_pairs,
    tno_width,
    pair_width,
    pair_coeff,
    pair_amps,
    pair_exch,
    tno_coeff,
    int_left,
    int_right,
    singles,
    tno_energy,
    gap,
):
    owner_count = lax.axis_size("pair")
    replica, me = lax.axis_index("rep"), lax.axis_index("pair")
    pair_dev, pno, domain = pair_coeff.shape
    trips, tno = tno_coeff.shape[0], tno_coeff.shape[2]
    ref_count = 3 * trips
    capacity = (2 * ref_count + owner_count - 1) // owner_count

    flat = triplet_pairs.reshape(1, ref_count)
    flat = jnp.pad(flat, ((0, 0), (0, padded_to(ref_count) - ref_count)))
    ids = share(flat, 0)[:, 0, :ref_count].reshape(owner_count, 2 * ref_count)
    mine = (ids // pair_dev == me).astype(jnp.float32)
    spot = jnp.arange(2 * ref_count, dtype=jnp.int32)
    before = (spot[:, None] < spot[None, :]).astype(jnp.float32)
    rank = jnp.dot(mine, before)
    slots = jnp.arange(capacity, dtype=jnp.int32).astype(jnp.float32)
    chosen = (mine[:, None, :] > 0) & (rank[:, None, :] == slots[None, :, None])
    rows = jnp.sum(jnp.where(chosen, (ids % pair_dev)[:, None, :], 0), axis=2).reshape(-1)

    inside = jnp.arange(pno, dtype=jnp.int32)[None, :] < pair_width[:, None]
    square = inside[:, :, None] & inside[:, None, :]
    block = jnp.where(square, jnp.where(replica == 0, pair_amps, pair_exch), 0)
    block = jnp.concatenate([block[:, :pno // 2], block[:, pno // 2:]], axis=2)
    send_block = block[rows].reshape(owner_count, capacity, pno // 2, 2 * pno)
    send_coeff = gather_rows(pair_coeff, rows, replica)
    send_coeff = send_coeff.reshape(owner_count, capacity, pno, domain // 2)
    got_coeff, got_block = exchange(send_coeff, send_block, 1)

    chip_refs = lax.dynamic_index_in_dim(ids, me, 0, keepdims=False)
    owners = chip_refs // pair_dev
    earlier = (owners[:, None] == owners[None, :]) & (spot[None, :] < spot[:, None])
    positions = owners * capacity + jnp.sum(earlier.astype(jnp.int32), axis=1)
    positions = lax.dynamic_slice_in_dim(positions, replica * ref_count, ref_count)
    energies = triplet_energies(
        positions,
        tno_width,
        got_coeff.reshape(2, -1, pno, domain // 2),
        got_block.reshape(2, -1, pno // 2, 2 * pno),
        tno_coeff, int_left, int_right, singles, tno_energy, gap,
    )
    everyone = share(energies, 2)[:, 0, :trips].reshape(-1)
    owned = jnp.arange(pair_dev, dtype=jnp.int32) + me * pair_dev
    shares = jnp.repeat(everyone / 3.0, 3)
    pair_energy = jnp.sum(
        jnp.where(ids.reshape(-1)[None, :] == owned[:, None], shares[None, :], 0.0), axis=1
    )
    return (energies[0, :trips], pair_energy)


def solution(mesh):
    placed = (
        P(("pair", "rep"), None),
        P(("pair", "rep")),
        P("pair"),
        P("pair", None, None),
        P("pair", None, None),
        P("pair", None, None),
        P(("pair", "rep"), None, None),
        P(("pair", "rep"), None, None, None),
        P(("pair", "rep"), None, None, None),
        P(("pair", "rep"), None, None),
        P(("pair", "rep"), None),
        P(("pair", "rep")),
    )
    return jax.shard_map(
        body, mesh=mesh, in_specs=placed, out_specs=(P(("pair", "rep")), P("pair")), check_vma=False
    )
```

```python
import functools

import jax
import jax.numpy as jnp
from jax import lax
from jax.experimental import pallas as pl
from jax.experimental.pallas import tpu as pltpu
from jax.sharding import PartitionSpec as P

GROUP = 8
ROW_STEP = 16


def triplet_kernel(
    pos_ref, width_ref, gap_ref, level_ref, single_ref,
    c0, c1, c2, p0, p1, p2, tno_ref, left_ref, right_ref, sing_ref, energy_ref,
    out_ref, lt_ref, at_ref, rm_ref, base_ref, s2_ref, x0_ref, x1_ref, x2_ref, acc_ref, even_ref, odd_ref,
):
    t = pl.program_id(0)
    width = width_ref[t]
    pno, tno = c0.shape[2], tno_ref.shape[2]
    half_dom = c0.shape[3]
    kept = lax.broadcasted_iota(jnp.int32, (1, tno), 1) < width
    keep = kept.astype(jnp.float32)
    keep_b = keep.astype(jnp.bfloat16)
    inter = sum(
        jnp.dot(
            jnp.concatenate([c0[h, 0], c1[h, 0], c2[h, 0]], axis=0),
            tno_ref[0, h * half_dom:(h + 1) * half_dom],
            preferred_element_type=jnp.float32,
        )
        for h in range(2)
    )
    inter = (inter * keep).astype(jnp.bfloat16)
    for x, blocks in enumerate((p0, p1, p2)):
        own = inter[x * pno:(x + 1) * pno]
        pair = jnp.concatenate(
            [
                jnp.concatenate([blocks[h, 0, :, :pno], blocks[h, 0, :, pno:]], axis=0)
                for h in range(2)
            ],
            axis=1,
        )
        half = lax.dot_general(
            own, pair, (((0,), (0,)), ((), ())), preferred_element_type=jnp.float32
        ).astype(jnp.bfloat16)
        amps = jnp.dot(half[:, :pno], own, preferred_element_type=jnp.float32)
        exch = jnp.dot(half[:, pno:], own, preferred_element_type=jnp.float32)
        cols = slice(x * tno, (x + 1) * tno)
        at_ref[:, cols] = amps.astype(jnp.bfloat16)
        (x0_ref, x1_ref, x2_ref)[x][...] = exch
        lt_ref[:, cols] = jnp.transpose(left_ref[0, x].astype(jnp.float32) * keep)
        rm_ref[cols, :] = right_ref[0, x] * keep_b
    levels = energy_ref[0]
    base_ref[...] = (
        jnp.transpose(jnp.broadcast_to(levels, (tno, tno))) + levels + gap_ref[t]
    )
    s2_ref[...] = jnp.transpose(jnp.broadcast_to(sing_ref[0, 2:3], (tno, tno)))
    acc_ref[...] = jnp.zeros_like(acc_ref)

    for low in range(tno // 2, tno + 1, ROW_STEP):
        fits = width <= low
        if low > tno // 2:
            fits = fits & (width > low - ROW_STEP)

        @pl.when(fits)
        def _(low=low):
            contract(
                low, t, width, level_ref, single_ref, sing_ref, lt_ref, at_ref, rm_ref,
                base_ref, s2_ref, x0_ref, x1_ref, x2_ref, acc_ref, even_ref, odd_ref,
            )

    @pl.when(t == 0)
    def _():
        out_ref[...] = jnp.zeros_like(out_ref)

    here = lax.broadcasted_iota(jnp.int32, out_ref.shape, 1) == t
    out_ref[...] = jnp.where(here, jnp.sum(acc_ref[...]), out_ref[...])


def contract(
    low, t, width, level_ref, single_ref, sing_ref, lt_ref, at_ref, rm_ref,
    base_ref, s2_ref, x0_ref, x1_ref, x2_ref, acc_ref, even_ref, odd_ref,
):
    tno = rm_ref.shape[1]
    groups = (width + GROUP - 1) // GROUP

    def multiply(g, conn_ref):
        first = pl.multiple_of(jnp.minimum(g, tno // GROUP - 1) * GROUP, GROUP)
        rows = lt_ref[pl.ds(first, GROUP), :]
        at = at_ref[:low]
        scaled = [
            at * jnp.broadcast_to(rows[j:j + 1], at.shape).astype(jnp.bfloat16)
            for j in range(GROUP)
        ]
        conn_ref[:GROUP * low] = jnp.dot(
            jnp.concatenate(scaled, axis=0), rm_ref[...], preferred_element_type=jnp.float32
        )

    def finish(g, conn_ref):
        first = pl.multiple_of(g * GROUP, GROUP)
        x2 = x2_ref[pl.ds(first, GROUP), :]
        x0 = x0_ref[:low]
        s0 = sing_ref[0, 0:1]
        total = acc_ref[...]
        for j in range(GROUP):
            part = conn_ref[j * low:(j + 1) * low]
            full = part + x0[:, j:j + 1] * s0
            full = full + single_ref[t, first + j] * x1_ref[:low]
            full = full + s2_ref[:low] * x2[j:j + 1]
            term = part * full / (base_ref[:low] + level_ref[t, first + j])
            total = total + jnp.sum(term.reshape(low // 8, 8, tno), axis=0)
        acc_ref[...] = total
        x0_ref[:low] = pltpu.roll(x0, tno - GROUP, 1)

    multiply(0, even_ref)

    @pl.loop(0, (groups + 1) // 2)
    def _(h):
        multiply(2 * h + 1, odd_ref)
        finish(2 * h, even_ref)
        multiply(2 * h + 2, even_ref)
        finish(2 * h + 1, odd_ref)


def padded_to(size):
    return (size + 127) // 128 * 128


def triplet_energies(
    positions, widths, flat_coeff, flat_paired, tno_coeff, left, right, singles, levels, gap
):
    trips, domain, tno = tno_coeff.shape
    pno = flat_coeff.shape[2]

    def pair_spec(shape, x):
        return pl.BlockSpec((2, 1) + shape, lambda t, pos, *_: (0, pos[t * 3 + x], 0, 0))

    def own_spec(shape):
        return pl.BlockSpec((1,) + shape, lambda t, *_: (t,) + (0,) * len(shape))

    out = pl.pallas_call(
        triplet_kernel,
        out_shape=jax.ShapeDtypeStruct((1, padded_to(trips)), jnp.float32),
        grid_spec=pltpu.PrefetchScalarGridSpec(
            num_scalar_prefetch=5,
            grid=(trips,),
            in_specs=[pair_spec((pno, domain // 2), x) for x in range(3)]
            + [pair_spec((pno // 2, 2 * pno), x) for x in range(3)]
            + [
                own_spec((domain, tno)),
                own_spec((3, tno, tno)),
                own_spec((3, tno, tno)),
                own_spec((3, tno)),
                own_spec((1, tno)),
            ],
            out_specs=pl.BlockSpec((1, padded_to(trips)), lambda t, *_: (0, 0)),
            scratch_shapes=[
                pltpu.VMEM((tno, 3 * tno), jnp.float32),
                pltpu.VMEM((tno, 3 * tno), jnp.bfloat16),
                pltpu.VMEM((3 * tno, tno), jnp.bfloat16),
            ]
            + [pltpu.VMEM((tno, tno), jnp.float32)] * 5
            + [pltpu.VMEM((8, tno), jnp.float32)]
            + [pltpu.VMEM((GROUP * tno, tno), jnp.float32)] * 2,
        ),
        compiler_params=pltpu.CompilerParams(dimension_semantics=("arbitrary",)),
        name="triplets",
    )(
        positions, widths, gap, levels, singles[:, 1],
        flat_coeff, flat_coeff, flat_coeff, flat_paired, flat_paired, flat_paired,
        tno_coeff, left, right, singles, levels[:, None, :],
    )
    return out


MESH = pl.DeviceIdType.MESH


def share_kernel(count, reps, x_ref, out_ref, send_sem, recv_sem):
    me = lax.axis_index("pair") * reps + lax.axis_index("rep")
    barrier = pltpu.get_barrier_semaphore()

    @pl.loop(1, count)
    def _(d):
        other = lax.rem(me + d, count)
        pl.semaphore_signal(
            barrier, inc=1, device_id=(other // reps, lax.rem(other, reps)), device_id_type=MESH
        )

    pl.semaphore_wait(barrier, count - 1)

    def copy(d):
        other = lax.rem(me + d, count)
        return pltpu.make_async_remote_copy(
            src_ref=x_ref,
            dst_ref=out_ref.at[me],
            send_sem=send_sem.at[d - 1],
            recv_sem=recv_sem.at[d - 1],
            device_id=(other // reps, lax.rem(other, reps)),
            device_id_type=MESH,
        )

    @pl.loop(1, count)
    def _(d):
        copy(d).start()

    out_ref[me] = x_ref[...]

    @pl.loop(1, count)
    def _(d):
        copy(d).wait()


def share(block, cid):
    owners, reps = lax.axis_size("pair"), lax.axis_size("rep")
    count = owners * reps
    return pl.pallas_call(
        functools.partial(share_kernel, count, reps),
        out_shape=jax.ShapeDtypeStruct((count,) + block.shape, block.dtype),
        in_specs=[pl.BlockSpec(memory_space=pltpu.VMEM)],
        out_specs=pl.BlockSpec(memory_space=pltpu.VMEM),
        scratch_shapes=[
            pltpu.SemaphoreType.DMA((count - 1,)),
            pltpu.SemaphoreType.DMA((count - 1,)),
        ],
        compiler_params=pltpu.CompilerParams(collective_id=cid, has_side_effects=True),
        name="share" + str(cid),
    )(block)


def partner(me, d, count, sign=1):
    if count & (count - 1):
        return lax.rem(me + sign * d + count, count)
    other, bit = me, 1
    while bit < count:
        if d & bit:
            other = other + bit * (1 - 2 * lax.rem(me // bit, 2))
        bit *= 2
    return other


def exchange_kernel(
    count, coeff_ref, block_ref, got_coeff, got_block,
    keep_coeff, keep_block, send_sem, recv_sem, pass_sem, land_sem, local_sem,
):
    me, rep = lax.axis_index("pair"), lax.axis_index("rep")
    sibling = (me, 1 - rep)
    barrier = pltpu.get_barrier_semaphore()
    pl.semaphore_signal(barrier, inc=1, device_id=sibling, device_id_type=MESH)

    @pl.loop(1, count)
    def _(d):
        pl.semaphore_signal(
            barrier, inc=1, device_id=(lax.rem(me + d, count), rep), device_id_type=MESH
        )

    pl.semaphore_wait(barrier, count)

    def send(d, k):
        other = partner(me, d, count)
        return pltpu.make_async_remote_copy(
            src_ref=(coeff_ref, block_ref)[k].at[other],
            dst_ref=(got_coeff, got_block)[k].at[rep, me],
            send_sem=send_sem.at[k, d - 1],
            recv_sem=recv_sem.at[k, d - 1],
            device_id=(other, rep),
            device_id_type=MESH,
        )

    def forward(d, k):
        origin = partner(me, d, count, -1)
        return pltpu.make_async_remote_copy(
            src_ref=(got_coeff, got_block)[k].at[rep, origin],
            dst_ref=(got_coeff, got_block)[k].at[rep, origin],
            send_sem=pass_sem.at[k, d],
            recv_sem=land_sem.at[k, d],
            device_id=sibling,
            device_id_type=MESH,
        )

    far_first = []
    for i, d in enumerate(range(count - 1, count // 2 - 1, -1)):
        far_first.append(d)
        if i % 2 and count // 2 - 1 - i // 2 > 0:
            far_first.append(count // 2 - 1 - i // 2)
    far_first += [d for d in range(count // 2 - 1, 0, -1) if d not in far_first]
    for d in far_first:
        for k in (1, 0):
            send(d, k).start()

    own = []
    for k in range(2):
        source, held = (coeff_ref, block_ref)[k], (keep_coeff, keep_block)[k]
        target = (got_coeff, got_block)[k]
        own.append((
            pltpu.make_async_copy(source.at[me], held, local_sem.at[k, 0]),
            pltpu.make_async_copy(held, target.at[rep, me], local_sem.at[k, 1]),
        ))
    for load, _ in own:
        load.start()
    for load, store in own:
        load.wait()
        store.start()
    for _, store in own:
        store.wait()
    for k in range(2):
        forward(0, k).start()
    for d in far_first[::-1]:
        for k in (1, 0):
            send(d, k).wait_recv()
            forward(d, k).start()

    for d in range(count):
        for k in range(2):
            if d:
                send(d, k).wait_send()
            forward(d, k).wait()


def exchange(coeff, block, cid):
    count = coeff.shape[0]
    shapes = [jax.ShapeDtypeStruct((2,) + a.shape, a.dtype) for a in (coeff, block)]
    return pl.pallas_call(
        functools.partial(exchange_kernel, count),
        out_shape=shapes,
        in_specs=[pl.BlockSpec(memory_space=pl.ANY)] * 2,
        out_specs=[pl.BlockSpec(memory_space=pl.ANY)] * 2,
        scratch_shapes=[
            pltpu.VMEM(coeff.shape[1:], coeff.dtype),
            pltpu.VMEM(block.shape[1:], block.dtype),
            pltpu.SemaphoreType.DMA((2, count - 1)),
            pltpu.SemaphoreType.DMA((2, count - 1)),
            pltpu.SemaphoreType.DMA((2, count)),
            pltpu.SemaphoreType.DMA((2, count)),
            pltpu.SemaphoreType.DMA((2, 2)),
        ],
        compiler_params=pltpu.CompilerParams(collective_id=cid, has_side_effects=True),
        name="exchange",
    )(coeff, block)


def gather_kernel(row_ref, rep_ref, coeff_ref, out_ref, held, in_sem, out_sem):
    total, _, half = held.shape
    start = pl.multiple_of(rep_ref[0] * half, half)

    def load(i):
        return pltpu.make_async_copy(
            coeff_ref.at[row_ref[i], :, pl.ds(start, half)], held.at[i], in_sem.at[i]
        )

    def store(i):
        return pltpu.make_async_copy(held.at[i], out_ref.at[i], out_sem.at[i])

    @pl.loop(0, total)
    def _(i):
        load(i).start()

    @pl.loop(0, total)
    def _(i):
        load(i).wait()
        store(i).start()

    @pl.loop(0, total)
    def _(i):
        store(i).wait()


def gather_rows(coeff, rows, rep):
    _, pno, domain = coeff.shape
    total = rows.shape[0]
    return pl.pallas_call(
        gather_kernel,
        out_shape=jax.ShapeDtypeStruct((total, pno, domain // 2), coeff.dtype),
        grid_spec=pltpu.PrefetchScalarGridSpec(
            num_scalar_prefetch=2,
            grid=(),
            in_specs=[pl.BlockSpec(memory_space=pl.ANY)],
            out_specs=pl.BlockSpec(memory_space=pl.ANY),
            scratch_shapes=[
                pltpu.VMEM((total, pno, domain // 2), coeff.dtype),
                pltpu.SemaphoreType.DMA((total,)),
                pltpu.SemaphoreType.DMA((total,)),
            ],
        ),
        name="gather_rows",
    )(rows, rep.reshape(1), coeff)


def body(
    triplet_pairs,
    tno_width,
    pair_width,
    pair_coeff,
    pair_amps,
    pair_exch,
    tno_coeff,
    int_left,
    int_right,
    singles,
    tno_energy,
    gap,
):
    owner_count = lax.axis_size("pair")
    replica, me = lax.axis_index("rep"), lax.axis_index("pair")
    pair_dev, pno, domain = pair_coeff.shape
    trips, tno = tno_coeff.shape[0], tno_coeff.shape[2]
    ref_count = 3 * trips
    capacity = (2 * ref_count + owner_count - 1) // owner_count

    flat = triplet_pairs.reshape(1, ref_count)
    flat = jnp.pad(flat, ((0, 0), (0, padded_to(ref_count) - ref_count)))
    ids = share(flat, 0)[:, 0, :ref_count].reshape(owner_count, 2 * ref_count)
    mine = (ids // pair_dev == me).astype(jnp.float32)
    spot = jnp.arange(2 * ref_count, dtype=jnp.int32)
    before = (spot[:, None] < spot[None, :]).astype(jnp.float32)
    rank = jnp.dot(mine, before)
    slots = jnp.arange(capacity, dtype=jnp.int32).astype(jnp.float32)
    chosen = (mine[:, None, :] > 0) & (rank[:, None, :] == slots[None, :, None])
    rows = jnp.sum(jnp.where(chosen, (ids % pair_dev)[:, None, :], 0), axis=2).reshape(-1)

    inside = jnp.arange(pno, dtype=jnp.int32)[None, :] < pair_width[:, None]
    square = inside[:, :, None] & inside[:, None, :]
    block = jnp.where(square, jnp.where(replica == 0, pair_amps, pair_exch), 0)
    block = jnp.concatenate([block[:, :pno // 2], block[:, pno // 2:]], axis=2)
    send_block = block[rows].reshape(owner_count, capacity, pno // 2, 2 * pno)
    send_coeff = gather_rows(pair_coeff, rows, replica)
    send_coeff = send_coeff.reshape(owner_count, capacity, pno, domain // 2)
    got_coeff, got_block = exchange(send_coeff, send_block, 1)

    chip_refs = lax.dynamic_index_in_dim(ids, me, 0, keepdims=False)
    owners = chip_refs // pair_dev
    earlier = (owners[:, None] == owners[None, :]) & (spot[None, :] < spot[:, None])
    positions = owners * capacity + jnp.sum(earlier.astype(jnp.int32), axis=1)
    positions = lax.dynamic_slice_in_dim(positions, replica * ref_count, ref_count)
    energies = triplet_energies(
        positions,
        tno_width,
        got_coeff.reshape(2, -1, pno, domain // 2),
        got_block.reshape(2, -1, pno // 2, 2 * pno),
        tno_coeff, int_left, int_right, singles, tno_energy, gap,
    )
    everyone = share(energies, 2)[:, 0, :trips].reshape(-1)
    owned = jnp.arange(pair_dev, dtype=jnp.int32) + me * pair_dev
    shares = jnp.repeat(everyone / 3.0, 3)
    pair_energy = jnp.sum(
        jnp.where(ids.reshape(-1)[None, :] == owned[:, None], shares[None, :], 0.0), axis=1
    )
    return (energies[0, :trips], pair_energy)


def solution(mesh):
    placed = (
        P(("pair", "rep"), None),
        P(("pair", "rep")),
        P("pair"),
        P("pair", None, None),
        P("pair", None, None),
        P("pair", None, None),
        P(("pair", "rep"), None, None),
        P(("pair", "rep"), None, None, None),
        P(("pair", "rep"), None, None, None),
        P(("pair", "rep"), None, None),
        P(("pair", "rep"), None),
        P(("pair", "rep")),
    )
    return jax.shard_map(
        body, mesh=mesh, in_specs=placed, out_specs=(P(("pair", "rep")), P("pair")), check_vma=False
    )
```
